32 devices in a mesh: row: 4 (over x, core), col: 4 (over z), pt: 2 (over y).
Axes of the slice: x: 2, y: 2, z: 4, core: 2. Of those that a mesh axis runs over, the one named last changes fastest.
Arguments:
- first_factors: int32 [32, 1024, 1024], P('pt', 'row', 'col'), may hold values from 0 to 12288
- second_factors: int32 [32, 1024, 1024], P('pt', 'row', 'col'), may hold values from 0 to 12288
Outputs:
- scaled_product: float32 [45, 1024, 1024], P(None, ('row', 'pt'), 'col')
The draws below stay inside these ranges and needn't reach their ends.
All inputs are finite; a program needn't handle non-finite values.
Results may differ from the reference program's by a relative error of at most 0.0003.
Values may be sent and summed in bfloat16 or wider, within the bound.
A program may use at most 128 MiB of HBM per device.

```python
import jax
import jax.numpy as jnp
import numpy as np
from jax import lax

N = 1024
DEG = 16


def touch_ends(result, stream_key, low, top_value):
    place = [jax.random.randint(jax.random.fold_in(stream_key, axis), (), 0, length) for axis, length in enumerate(result.shape)]
    longest = result.shape.index(max(result.shape))
    neighbour = place[:longest] + [(place[longest] + 1) % result.shape[longest]] + place[longest + 1:]
    return result.at[tuple(place)].set(low).at[tuple(neighbour)].set(top_value)


def setup_inputs(seed: int = 0) -> dict:
    key_of = jax.random.split(jax.random.key(seed), 3)
    return {
        "first_factors": touch_ends(jax.random.randint(key_of[0], (2 * DEG, N, N), 0, 12289), jax.random.fold_in(key_of[0], 1), 0, 12288).astype(jnp.int32),
        "second_factors": touch_ends(jax.random.randint(key_of[1], (2 * DEG, N, N), 0, 12289), jax.random.fold_in(key_of[1], 1), 0, 12288).astype(jnp.int32),
    }


modulus = 12289
digit_base = 128


def primitive_root():
    for candidate in range(2, modulus):
        if pow(candidate, 6144, modulus) != 1 and pow(candidate, 4096, modulus) != 1:
            return candidate
    return 0


def make_table(order_size, row_count, column_count, inverse):
    generator = primitive_root()
    root_value = pow(generator, (modulus - 1) // order_size, modulus)
    scaling = 1
    if inverse:
        root_value = pow(root_value, modulus - 2, modulus)
        scaling = pow(order_size, modulus - 2, modulus)
    entries = [[pow(root_value, (row_index * column_index) % order_size, modulus) * scaling % modulus
                for column_index in range(column_count)] for row_index in range(row_count)]
    return np.array(entries, dtype=np.int64)


def exact_dot(left_part, right_part):
    return jnp.dot(left_part, right_part, precision=lax.Precision.HIGHEST, preferred_element_type=jnp.float32)


def value_digits(values):
    high_digit = values // digit_base
    return high_digit.astype(jnp.float32), (values - digit_base * high_digit).astype(jnp.float32)


def combine(high_high, high_low, low_high, low_low):
    top_part = high_high.astype(jnp.int32) % modulus
    middle_part = (high_low.astype(jnp.int32) + low_high.astype(jnp.int32)) % modulus
    return ((top_part * (digit_base * digit_base)) % modulus + middle_part * digit_base + low_low.astype(jnp.int32)) % modulus


def modular_product(matrix_table, values):
    table_high = jnp.asarray(matrix_table // digit_base, dtype=jnp.float32)
    table_low = jnp.asarray(matrix_table % digit_base, dtype=jnp.float32)
    data_high, data_low = value_digits(values)
    return combine(exact_dot(table_high, data_high), exact_dot(table_high, data_low),
                   exact_dot(table_low, data_high), exact_dot(table_low, data_low))


def transform(matrix_table, coefs):
    slot_count = coefs.shape[0]
    blocks = coefs.reshape(slot_count, 16, coefs.shape[1] // 16, coefs.shape[2]).transpose(1, 0, 2, 3)

    def one_block(block):
        flat_coefs = block.reshape(slot_count, -1)
        return modular_product(matrix_table, flat_coefs).reshape(-1, block.shape[1], block.shape[2])

    mapped = lax.map(one_block, blocks)
    return mapped.transpose(1, 0, 2, 3).reshape(-1, coefs.shape[1], coefs.shape[2])


def pointwise(left_values, right_values):
    def one_point(pair_in):
        left_high, left_low = value_digits(pair_in[0])
        right_high, right_low = value_digits(pair_in[1])
        return combine(exact_dot(left_high, right_high), exact_dot(left_high, right_low),
                       exact_dot(left_low, right_high), exact_dot(left_low, right_low))

    return lax.map(one_point, (left_values, right_values))


def reference(first_factors, second_factors):
    forward_one = make_table(2 * DEG, 2 * DEG, DEG, False)
    inverse_one = make_table(2 * DEG, 2 * DEG, 2 * DEG, True)
    forward_two = make_table(4 * DEG, 4 * DEG, 2 * DEG, False)
    inverse_two = make_table(4 * DEG, 3 * DEG - 3, 4 * DEG, True)
    left_values = jnp.concatenate([transform(forward_one, first_factors[:DEG]),
                                   transform(forward_one, first_factors[DEG:])], 0)
    right_values = jnp.concatenate([transform(forward_one, second_factors[:DEG]),
                                    transform(forward_one, second_factors[DEG:])], 0)
    products = pointwise(left_values, right_values)
    first_product = transform(inverse_one, products[:2 * DEG])
    second_product = transform(inverse_one, products[2 * DEG:])
    upper_values = transform(forward_two, first_product)
    lower_values = transform(forward_two[:, :DEG], second_product[DEG:])
    result_coefficients = transform(inverse_two, pointwise(upper_values, lower_values))
    return result_coefficients.astype(jnp.float32) / 12289.0
```

```python
import jax
import jax.numpy as jnp
import numpy as np
from jax import lax
from jax.sharding import PartitionSpec as P

DEG = 16


modulus = 12289
digit_base = 128


def primitive_root():
    for candidate in range(2, modulus):
        if pow(candidate, 6144, modulus) != 1 and pow(candidate, 4096, modulus) != 1:
            return candidate
    return 0


def make_table(order_size, row_count, column_count, inverse):
    generator = primitive_root()
    root_value = pow(generator, (modulus - 1) // order_size, modulus)
    scaling = 1
    if inverse:
        root_value = pow(root_value, modulus - 2, modulus)
        scaling = pow(order_size, modulus - 2, modulus)
    entries = [
        [
            pow(root_value, row_index * column_index % order_size, modulus) * scaling % modulus
            for column_index in range(column_count)
        ]
        for row_index in range(row_count)
    ]
    return np.array(entries, dtype=np.int64)


def value_digits(values):
    high_digit = values // digit_base
    return (
        high_digit.astype(jnp.bfloat16),
        (values - digit_base * high_digit).astype(jnp.bfloat16),
    )


def combine(high_high, high_low, low_high, low_low):
    top_part = high_high.astype(jnp.int32) % modulus
    middle_part = (high_low.astype(jnp.int32) + low_high.astype(jnp.int32)) % modulus
    return (
        top_part * (digit_base * digit_base) % modulus
        + middle_part * digit_base
        + low_low.astype(jnp.int32)
    ) % modulus


def transform(matrix_table, coefs):
    slot_count = coefs.shape[0]
    flat_coefs = coefs.reshape(slot_count, -1)
    table_high = jnp.asarray(matrix_table // digit_base, dtype=jnp.bfloat16)
    table_low = jnp.asarray(matrix_table % digit_base, dtype=jnp.bfloat16)
    data_high, data_low = value_digits(flat_coefs)

    def product_of(left_part, right_part):
        return jnp.dot(left_part, right_part, preferred_element_type=jnp.float32)

    mixed_values = combine(
        product_of(table_high, data_high),
        product_of(table_high, data_low),
        product_of(table_low, data_high),
        product_of(table_low, data_low),
    )
    return mixed_values.reshape(matrix_table.shape[0], coefs.shape[1], coefs.shape[2])


def batched_product(left_part, right_part):
    return jnp.einsum("bik,bkj->bij", left_part, right_part, preferred_element_type=jnp.float32)


def digit_sum(totals, left_digits, right_digits):
    return (
        totals[0] + batched_product(left_digits[0], right_digits[0]),
        totals[1] + batched_product(left_digits[0], right_digits[1]),
        totals[2] + batched_product(left_digits[1], right_digits[0]),
        totals[3] + batched_product(left_digits[1], right_digits[1]),
    )


def pointwise(left_values, right_values):
    left_points, right_points = (
        lax.all_to_all(
            lax.all_to_all(
                left_values.astype(jnp.float32), "col", split_axis=0, concat_axis=2, tiled=True
            ),
            "pt",
            split_axis=0,
            concat_axis=1,
            tiled=True,
        ),
        lax.all_to_all(
            lax.all_to_all(
                right_values.astype(jnp.float32), "col", split_axis=0, concat_axis=2, tiled=True
            ),
            "pt",
            split_axis=0,
            concat_axis=1,
            tiled=True,
        ),
    )
    left_digits = value_digits(left_points.astype(jnp.int32))
    right_digits = value_digits(right_points.astype(jnp.int32))
    zeros_init = jnp.zeros(left_points.shape, jnp.float32)
    column_parts = tuple((digit_part for digit_part in left_digits))
    totals = digit_sum(
        (zeros_init, zeros_init, zeros_init, zeros_init),
        column_parts,
        (
            lax.all_gather(right_digits[0], "row", axis=1, tiled=True),
            lax.all_gather(right_digits[1], "row", axis=1, tiled=True),
        ),
    )
    product_values = combine(totals[0], totals[1], totals[2], totals[3]).astype(jnp.float32)
    arrived = lax.all_to_all(
        lax.all_to_all(product_values, "col", split_axis=2, concat_axis=0, tiled=True),
        "pt",
        split_axis=1,
        concat_axis=0,
        tiled=True,
    )
    col_count = lax.axis_size("col")
    pt_count = lax.axis_size("pt")
    local_count = arrived.shape[0] // (col_count * pt_count)
    returned = arrived.reshape(pt_count, col_count, local_count, arrived.shape[1], arrived.shape[2])
    returned = returned.transpose(1, 0, 2, 3, 4).reshape(arrived.shape)
    return returned.astype(jnp.int32)


def local(first_factors, second_factors):
    forward_one = make_table(2 * DEG, 2 * DEG, DEG, False)
    inverse_one = make_table(2 * DEG, 2 * DEG, 2 * DEG, True)
    forward_two = make_table(4 * DEG, 4 * DEG, 2 * DEG, False)
    inverse_two = make_table(4 * DEG, 3 * DEG - 3, 4 * DEG, True)
    first_entries, second_entries = (
        lax.all_to_all(
            first_factors.astype(jnp.float32), "pt", split_axis=1, concat_axis=0, tiled=True
        ),
        lax.all_to_all(
            second_factors.astype(jnp.float32), "pt", split_axis=1, concat_axis=0, tiled=True
        ),
    )
    first_entries = first_entries.astype(jnp.int32)
    second_entries = second_entries.astype(jnp.int32)
    left_values = jnp.concatenate(
        [transform(forward_one, first_entries[:DEG]), transform(forward_one, first_entries[DEG:])],
        0,
    )
    right_values = jnp.concatenate(
        [
            transform(forward_one, second_entries[:DEG]),
            transform(forward_one, second_entries[DEG:]),
        ],
        0,
    )
    products = pointwise(left_values, right_values)
    first_product = transform(inverse_one, products[: 2 * DEG])
    second_product = transform(inverse_one, products[2 * DEG :])
    upper_values = transform(forward_two, first_product)
    lower_values = transform(forward_two[:, :DEG], second_product[DEG:])
    result_coefficients = transform(inverse_two, pointwise(upper_values, lower_values))
    return result_coefficients.astype(jnp.float32) / 12289.0


def reduce_centred(values):
    return values - 12289.0 * jnp.round(values * (1.0 / 12289.0))


def centred_digits(values):
    high_digit = jnp.round(values * (1.0 / 128.0))
    return high_digit.astype(jnp.bfloat16), (values - 128.0 * high_digit).astype(jnp.bfloat16)


def combine_centred(high_high, middle, low_low):
    upper_part = reduce_centred(reduce_centred(high_high) * 128.0 + middle)
    return reduce_centred(upper_part * 128.0 + low_low)


def table_digits(matrix_table):
    centred = np.where(matrix_table > modulus // 2, matrix_table - modulus, matrix_table)
    high_digit = np.round(centred / 128.0)
    return high_digit, centred - 128.0 * high_digit


def centred_transform(table_high, table_low, coefs):
    data_high, data_low = centred_digits(coefs.astype(jnp.float32))
    table_high = jnp.asarray(table_high, dtype=jnp.bfloat16)
    table_low = jnp.asarray(table_low, dtype=jnp.bfloat16)

    def product_of(left_part, right_part):
        return jnp.einsum("ts,sab->tab", left_part, right_part, preferred_element_type=jnp.float32)

    middle = product_of(
        jnp.concatenate([table_high, table_low], 1), jnp.concatenate([data_low, data_high], 0)
    )
    return combine_centred(
        product_of(table_high, data_high), middle, product_of(table_low, data_low)
    )


def column_pointwise(left_values, right_values):
    right_points = lax.all_to_all(
        right_values.astype(jnp.int16), "col", split_axis=0, concat_axis=2, tiled=True
    )
    right_points = lax.all_gather(right_points, "row", axis=1, tiled=True)
    left_points = lax.all_to_all(
        left_values.astype(jnp.int16), "col", split_axis=0, concat_axis=2, tiled=True
    )
    left_high, left_low = centred_digits(left_points.astype(jnp.float32))
    right_high, right_low = centred_digits(right_points.astype(jnp.float32))
    middle = batched_product(left_high, right_low) + batched_product(left_low, right_high)
    product_values = combine_centred(
        batched_product(left_high, right_high), middle, batched_product(left_low, right_low)
    )
    return lax.all_to_all(
        product_values.astype(jnp.int16), "col", split_axis=2, concat_axis=0, tiled=True
    )


def pair_local(first_factors, second_factors):
    forward_one = table_digits(make_table(2 * DEG, 2 * DEG, DEG, False))
    inverse_one = table_digits(make_table(2 * DEG, 2 * DEG, 2 * DEG, True))
    forward_two = table_digits(make_table(4 * DEG, 4 * DEG, 2 * DEG, False))
    inverse_two = table_digits(make_table(4 * DEG, 3 * DEG - 3, 4 * DEG, True))
    half_points = 2 * DEG
    place = lax.axis_index("pt")
    products = column_pointwise(
        centred_transform(*forward_one, centre(first_factors)),
        centred_transform(*forward_one, centre(second_factors)),
    )
    own_product = centred_transform(*inverse_one, products).astype(jnp.int16)
    both_products = lax.all_gather(own_product, "pt", axis=0, tiled=True)
    first_product = both_products[: 2 * DEG]
    shifted = both_products[3 * DEG :]
    own_tables = [
        lax.dynamic_slice_in_dim(
            jnp.asarray(digit, dtype=jnp.bfloat16), place * half_points, half_points, 0
        )
        for digit in forward_two
    ]
    upper_values = centred_transform(*own_tables, first_product)
    lower_values = centred_transform(*[digit[:, :DEG] for digit in own_tables], shifted)
    products_two = column_pointwise(upper_values, lower_values)
    all_points = lax.all_to_all(products_two, "pt", split_axis=1, concat_axis=0, tiled=True)
    result = centred_transform(*inverse_two, all_points)
    return jnp.where(result < 0.0, result + 12289.0, result) / 12289.0


def centre(values):
    return jnp.where(values > modulus // 2, values - modulus, values)


def solution(mesh):
    in_specs = (P("pt", "row", "col"), P("pt", "row", "col"))
    out_specs = P(None, ("row", "pt"), "col")
    body = pair_local if mesh.shape["pt"] == 2 else local
    return jax.shard_map(body, mesh=mesh, in_specs=in_specs, out_specs=out_specs, check_vma=False)
```
